32 devices in a mesh: section: 4 (over z), dom: 8 (over y, x, core).
Axes of the slice: x: 2, y: 2, z: 4, core: 2. Of those that a mesh axis runs over, the one named last changes fastest.
Arguments:
- top_grad: bfloat16 [1, 4096, 512], P(None, 'dom'), may hold values from -6 to 6
- agg_in: bfloat16 [4, 1, 4096, 512], P('section', None, 'dom'), may hold values from -6 to 6
- pre_act: bfloat16 [4, 1, 4096, 512], P('section', None, 'dom'), may hold values from -6 to 6
- weights: bfloat16 [4, 512, 512], P('section'), may hold values from -0.25 to 0.25
- local_adj_t: bfloat16 [1, 4096, 512], P(None, 'dom'), may hold values from -0.25 to 0.25
- tiles: bfloat16 [1, 24, 128, 128], P(None, 'dom'), may hold values from -0.625 to 0.625
- tile_source: int32 [1, 24], P(None, 'dom'), may hold values from 0 to 3
- owner_rows: int32 [1, 8, 8, 48], P(None, 'dom'), may hold values from 0 to 511, as said below
- counts: int32 [1, 8, 8], P(None, 'dom'), may hold values from 1 to 48, as said below
Outputs:
- layer_grads: bfloat16 [4, 1, 4096, 512], P('section', None, 'dom')
- weight_grads: float32 [4, 512, 512], P('section', 'dom')
The draws below stay inside these ranges and needn't reach their ends.
Inputs may be any that keep to these rules, and one draw needn't show every extreme that they name: `owner_rows`: distinct local nodes of the owner for the slots of one source; only the first counts slots are live. `counts`: in every group one owner part receives all 48 slots from every source part.
All inputs are finite; a program needn't handle non-finite values.
Results may differ from the reference program's by a relative error of at most 0.022.
Values may be sent and summed in bfloat16 or wider, within the bound.
A program may use at most 64 MiB of HBM per device.

```python
import math
import jax
import jax.numpy as jnp

F = 512
TILE = 128
CAPR = 48
ROWS = 512
GROUPS = 1
LAYERS = 4
NODES = 4096
MBLK = 3
N_DOM = 8


def draw_owner_rows(key, part):
    scores = jax.random.randint(key, (GROUPS, N_DOM, N_DOM, ROWS), 0, 1 << 20) * ROWS + jnp.arange(ROWS).astype(jnp.int32)
    ordered = jnp.argsort(scores, axis=-1)
    return ordered[..., :CAPR].astype(jnp.int32)


def draw_counts(key, part):
    key_low = jax.random.fold_in(key, 11)
    key_count = jax.random.fold_in(key, 12)
    key_hot = jax.random.fold_in(key, 13)
    lower = jax.random.randint(key_low, (GROUPS, N_DOM, 1), 1, CAPR // 2 + 1)
    drawn = jax.random.randint(key_count, (GROUPS, N_DOM, N_DOM), lower, CAPR + 1)
    hot_owner = jax.random.randint(key_hot, (GROUPS, 1, 1), 0, N_DOM)
    is_full = jnp.arange(N_DOM).astype(jnp.int32)[None, :, None] == hot_owner
    return jnp.where(is_full, CAPR, drawn).astype(jnp.int32)


def plant(result, key, least, high):
    extent = result.shape
    place = [jax.random.randint(jax.random.fold_in(key, axis), (), 0, extent[axis]) for axis in range(len(extent))]
    result = result.at[tuple(place)].set(least)
    longest = extent.index(max(extent))
    place[longest] = (place[longest] + 1) % extent[longest]
    return result.at[tuple(place)].set(high)


def raised(values, rng, source, target, parts, factor):
    owner, partner = [(jnp.arange(values.shape[axis_at]) // (values.shape[axis_at] // parts)).reshape([-1 if axis == axis_at else 1 for axis in range(values.ndim)]) for axis_at in (source, target)]
    chosen = jax.random.permutation(rng, parts)[partner]
    strong = (owner == chosen) | (owner == (partner + parts // 2) % parts)
    return jnp.where(strong, factor * values, values)


def block_scale(rng, shape, pieces, least, high):
    level, own = 1.0, jax.random.fold_in(rng, 6)
    for dim, parts in pieces:
        steps = jnp.exp(jax.random.uniform(jax.random.fold_in(own, dim), (parts,), jnp.float32, least / len(pieces), high / len(pieces)))
        level = level * jnp.repeat(steps, shape[dim] // parts).reshape([-1 if axis == dim else 1 for axis in range(len(shape))])
    return level


def normal_values(rng, shape, scale, bound, pieces=(), dtype=jnp.bfloat16):
    factor_of = block_scale(rng, shape, pieces, -0.22, 0.18) if pieces else 1.0
    values = jax.random.normal(rng, shape, jnp.float32) * scale * factor_of
    return jnp.minimum(jnp.maximum(values, -bound), bound).astype(dtype)


def gaussian_with(key, shape, scale, reach, pieces, heavy, held_as=jnp.bfloat16):
    array = scale * jax.random.normal(key, shape, jnp.float32)
    if pieces:
        array = array * block_scale(key, shape, pieces, -0.22, 0.18)
    return jnp.clip(raised(array, jax.random.fold_in(key, 3), *heavy), -reach, reach).astype(held_as)


def setup_inputs(seed: int = 0) -> dict:
    key_of = jax.random.split(jax.random.key(seed), 10)
    top_grad = normal_values(key_of[0], (GROUPS, NODES, F), 1.0, 6.0, ((1, 8),))
    agg_in = gaussian_with(key_of[1], (LAYERS, GROUPS, NODES, F), 1.0, 6.0, ((0, 4), (2, 8)), (2, 3, 8, 2.0))
    pre_act = normal_values(key_of[2], (LAYERS, GROUPS, NODES, F), 1.0, 6.0, ((0, 4), (2, 8)))
    weights = normal_values(key_of[3], (LAYERS, F, F), F ** -0.5, 0.25, ((0, 4),))
    local_adj_t = normal_values(key_of[4], (GROUPS, NODES, ROWS), ROWS ** -0.5, 0.25, ((1, 8),))
    tiles = normal_values(key_of[5], (GROUPS, N_DOM * MBLK, TILE, TILE), (TILE * N_DOM * CAPR // ROWS) ** -0.5, 0.625, ((1, 8),))
    tile_source = plant(jax.random.randint(key_of[6], (GROUPS, N_DOM * MBLK), 0, ROWS // TILE), jax.random.fold_in(key_of[6], 1), 0, (ROWS // TILE) - 1).astype(jnp.int32)
    owner_rows = draw_owner_rows(jax.random.fold_in(key_of[9], 71), 0)
    counts = draw_counts(jax.random.fold_in(key_of[9], 71), 0)
    return {"top_grad": top_grad, "agg_in": agg_in, "pre_act": pre_act, "weights": weights, "local_adj_t": local_adj_t, "tiles": tiles, "tile_source": tile_source, "owner_rows": owner_rows, "counts": counts}


def reference(top_grad, agg_in, pre_act, weights, local_adj_t, tiles, tile_source, owner_rows, counts):
    node_count = ROWS * N_DOM
    tile_blocks = N_DOM * CAPR // TILE
    scale_factor = 1.0 / math.sqrt(GROUPS * node_count)
    weight_acc = [jnp.zeros((F, F), jnp.float32) for layer_idx in range(LAYERS)]
    grads_table = [[None] * GROUPS for layer_idx in range(LAYERS)]
    source_part = (jnp.arange(N_DOM * tile_blocks) // tile_blocks).astype(jnp.int32)
    owner_base = (jnp.arange(N_DOM) * ROWS).astype(jnp.int32)
    slot_index = jnp.arange(CAPR).astype(jnp.int32)
    for group_idx in range(GROUPS):
        gradient = top_grad[group_idx]
        for layer_idx in reversed(range(LAYERS)):
            masked = jnp.where(pre_act[layer_idx, group_idx] > 0, gradient, jnp.zeros_like(gradient))
            weight_acc[layer_idx] = weight_acc[layer_idx] + jnp.dot(agg_in[layer_idx, group_idx].T, masked, preferred_element_type=jnp.float32)
            grad_y = jnp.dot(masked, weights[layer_idx].T, preferred_element_type=jnp.float32).astype(jnp.bfloat16)
            local_sum = jnp.einsum('ejk,ekf->ejf', local_adj_t[group_idx].reshape(N_DOM, ROWS, ROWS).astype(jnp.float32), grad_y.reshape(N_DOM, ROWS, F).astype(jnp.float32)).reshape(node_count, F)
            blocks_all = grad_y.reshape(node_count // TILE, TILE, F)
            block_pick = (source_part * (ROWS // TILE) + tile_source[group_idx]).astype(jnp.int32)
            picked = blocks_all[block_pick]
            mirror = jnp.einsum('brt,btf->brf', tiles[group_idx].astype(jnp.float32), picked.astype(jnp.float32)).astype(jnp.bfloat16)
            mirror = mirror.reshape(N_DOM, N_DOM, CAPR, F)
            targets = jnp.transpose(owner_rows[group_idx], (1, 0, 2))
            live_count = jnp.transpose(counts[group_idx], (1, 0))
            is_valid = slot_index[None, None, :] < live_count[:, :, None]
            global_rows = jnp.where(is_valid, owner_base[None, :, None] + targets, node_count).reshape(-1)
            boundary = jnp.zeros((node_count, F), jnp.float32).at[global_rows].add(mirror.reshape(-1, F).astype(jnp.float32), mode='drop')
            gradient = (local_sum + boundary).astype(jnp.bfloat16)
            grads_table[layer_idx][group_idx] = gradient
    layer_grads = jnp.stack([jnp.stack(grads_table[layer_idx], 0) for layer_idx in range(LAYERS)], 0)
    weight_grads = jnp.stack([weight_acc[layer_idx] * scale_factor for layer_idx in range(LAYERS)], 0)
    return (layer_grads, weight_grads)
```

```python
import functools
import math

import jax
import jax.numpy as jnp
from jax import lax
from jax.experimental import pallas as pl
from jax.experimental.pallas import tpu as pltpu
from jax.sharding import PartitionSpec as P

MESH = pl.DeviceIdType.MESH


def dot(a, b, dims=((1,), (0,))):
    return lax.dot_general(a, b, (dims, ((), ())), preferred_element_type=jnp.float32)


def kernel(
    sections, parts, chunk, scale,
    top, agg, pre, weight, adj, tiles, tile_source, target,
    out_grad, out_dw,
    gbuf, pbuf, wbuf, abuf, xbuf, tbuf, tfull, sbuf, zbuf, yacc, ybuf, lbuf, msend, mrecv,
    dwsend, dwown, dwrecv,
    load_sem, first_sem, zin_sem, zout_sem, feed_out, feed_in, msend_sem, mrecv_sem,
    dwsend_sem, dwrecv_sem,
):
    rows, feat = abuf.shape[0], zbuf.shape[1]
    chunks = feat // chunk
    slots = msend.shape[2] // parts
    tile_count, tile = tbuf.shape[0], tbuf.shape[1]
    shard = feat // parts
    sec = lax.axis_index("section")
    me = lax.axis_index("dom")
    top_sec = sections - 1
    is_top = sec == top_sec
    double = (lax.rem(sec, 2) == 0) & (sec < sections - 2)
    feeder = (lax.rem(sec, 2) == 1) & (sec < top_sec)
    passer = (sec > 0) & jnp.logical_not(feeder)
    begin = jnp.where(double, 0, 1)

    below = jnp.maximum(sec - 1, 0)
    below_slot = jnp.where((lax.rem(below, 2) == 0) & (below < sections - 2), 0, 1)

    loads = [
        pltpu.make_async_copy(weight.at[0], wbuf.at[1], load_sem.at[0]),
        pltpu.make_async_copy(pre.at[0, 0], pbuf.at[1], load_sem.at[1]),
        pltpu.make_async_copy(tiles.at[0], tbuf, load_sem.at[2]),
        pltpu.make_async_copy(adj.at[0], abuf, load_sem.at[3]),
        pltpu.make_async_copy(agg.at[0, 0], xbuf, load_sem.at[4]),
    ]

    def cols(c):
        return pl.ds(c * chunk, chunk)

    @pl.when(is_top)
    def _():
        for c in range(chunks):
            pltpu.make_async_copy(top.at[0, :, cols(c)], gbuf.at[1, c], first_sem.at[c]).start()

    for load in loads:
        load.start()

    barrier = pltpu.get_barrier_semaphore()
    for i in range(1, parts):
        pl.semaphore_signal(
            barrier, inc=1, device_id={"dom": lax.rem(me + i, parts)}, device_id_type=MESH
        )

    @pl.when(sec > 0)
    def _():
        pl.semaphore_signal(barrier, inc=1, device_id={"section": sec - 1}, device_id_type=MESH)

    @pl.when(sec < top_sec)
    def _():
        pl.semaphore_signal(barrier, inc=1, device_id={"section": sec + 1}, device_id_type=MESH)

    vertical = jnp.where(sec > 0, 1, 0) + jnp.where(sec < top_sec, 1, 0)
    pl.semaphore_wait(barrier, parts - 1 + vertical)

    def feed(i):
        source, dest = ((pre.at[0, 0], pbuf.at[0]), (weight.at[0], wbuf.at[0]))[i]
        return pltpu.make_async_remote_copy(
            src_ref=source, dst_ref=dest, send_sem=feed_out.at[i], recv_sem=feed_in.at[i],
            device_id={"section": below}, device_id_type=MESH,
        )

    @pl.when(feeder)
    def _():
        for i in range(2):
            feed(i).start()

    def pass_down(source_slot, c):
        return pltpu.make_async_remote_copy(
            src_ref=gbuf.at[source_slot, c], dst_ref=gbuf.at[below_slot, c],
            send_sem=zout_sem.at[c], recv_sem=zin_sem.at[c],
            device_id={"section": below}, device_id_type=MESH,
        )

    loads[2].wait()
    for b in range(tile_count):
        block = tbuf[b].astype(jnp.float32)
        for j in range(rows // tile):
            hit = (tile_source[0, b] == j).astype(jnp.float32)
            tfull[pl.ds(b * tile, tile), pl.ds(j * tile, tile)] = (block * hit).astype(jnp.bfloat16)
    loads[0].wait()
    loads[1].wait()
    loads[3].wait()

    def boundary_copy(phase, c, i):
        peer = lax.rem(me + i, parts)
        return pltpu.make_async_remote_copy(
            src_ref=msend.at[phase, c, pl.ds(pl.multiple_of(peer * slots, 16), slots)],
            dst_ref=mrecv.at[phase, c, pl.ds(pl.multiple_of(me * slots, 16), slots)],
            send_sem=msend_sem.at[phase, c, i - 1],
            recv_sem=mrecv_sem.at[phase, c, i - 1],
            device_id={"dom": peer}, device_id_type=MESH,
        )

    def boundary_arrived(phase, c, i):
        source = lax.rem(me + parts - i, parts)
        return pltpu.make_async_remote_copy(
            src_ref=msend.at[phase, c, pl.ds(pl.multiple_of(source * slots, 16), slots)],
            dst_ref=mrecv.at[phase, c, pl.ds(pl.multiple_of(source * slots, 16), slots)],
            send_sem=msend_sem.at[phase, c, i - 1],
            recv_sem=mrecv_sem.at[phase, c, i - 1],
            device_id={"dom": source}, device_id_type=MESH,
        )

    def dw_copy(i):
        peer = lax.rem(me + i, parts)
        return pltpu.make_async_remote_copy(
            src_ref=dwsend.at[peer], dst_ref=dwrecv.at[i - 1],
            send_sem=dwsend_sem.at[i - 1], recv_sem=dwrecv_sem.at[i - 1],
            device_id={"dom": peer}, device_id_type=MESH,
        )

    spot = lax.broadcasted_iota(jnp.int32, (rows, parts * slots), 0)
    sbuf[...] = jnp.where(spot == target[...], 1.0, 0.0).astype(jnp.bfloat16)

    def run_layer(phase, carry):
        @pl.when(phase == 0)
        def _():
            for i in range(2):
                feed(i).wait_recv()

        for c in range(chunks):
            @pl.when((phase == begin) & jnp.logical_not(is_top))
            def _():
                pass_down(1, c).wait_recv()

            @pl.when(is_top)
            def _():
                pltpu.make_async_copy(
                    top.at[0, :, cols(c)], gbuf.at[1, c], first_sem.at[c]
                ).wait()

            @pl.when(feeder)
            def _():
                pass_down(1, c).start()

            gradient = gbuf[phase, c].astype(jnp.float32)
            keep = pbuf[phase, :, cols(c)].astype(jnp.float32) > 0
            masked = jnp.where(keep, gradient, 0.0).astype(jnp.bfloat16)
            zbuf[:, cols(c)] = masked
            term = dot(masked, wbuf[phase, :, cols(c)], ((1,), (1,)))
            if c == 0:
                yacc[...] = term
            elif c < chunks - 1:
                yacc[...] += term
            else:
                ybuf[...] = (yacc[...] + term).astype(jnp.bfloat16)

        for c in range(chunks):
            msend[phase, c] = dot(tfull[...], ybuf[:, cols(c)]).astype(jnp.bfloat16)
            for i in range(1, parts):
                boundary_copy(phase, c, i).start()
            own = pl.ds(pl.multiple_of(me * slots, 16), slots)
            mrecv[phase, c, own, :] = msend[phase, c, own, :]

        for c in range(chunks):
            lbuf[c] = dot(abuf[...], ybuf[:, cols(c)])

        @pl.when(phase == 1)
        def _():
            loads[4].wait()
            for d in range(parts):
                part = dot(xbuf[:, pl.ds(d * shard, shard)], zbuf[...], ((0,), (0,)))
                dwsend[d] = part.astype(jnp.bfloat16)

                @pl.when(me == d)
                def _():
                    dwown[...] = part
            for i in range(1, parts):
                dw_copy(i).start()

        for c in range(chunks):
            for i in range(1, parts):
                boundary_arrived(phase, c, i).wait_recv()
            total = (lbuf[c] + dot(sbuf[...], mrecv[phase, c])).astype(jnp.bfloat16)
            gbuf[phase + 1, c] = total

            @pl.when(phase == 1)
            def _():
                @pl.when(passer)
                def _():
                    pass_down(2, c).start()

                out_grad[0, 0, :, cols(c)] = total

        for c in range(chunks):
            for i in range(1, parts):
                boundary_copy(phase, c, i).wait_send()
        return carry

    lax.fori_loop(begin, 2, run_layer, 0)

    total = dwown[...]
    for i in range(1, parts):
        dw_copy(i).wait_recv()
        total = total + dwrecv[i - 1].astype(jnp.float32)
    out_dw[0] = total * scale

    for i in range(1, parts):
        dw_copy(i).wait_send()

    @pl.when(sec > 0)
    def _():
        for c in range(chunks):
            pass_down(1, c).wait_send()

    @pl.when(feeder)
    def _():
        for i in range(2):
            feed(i).wait_send()


def per_device(
    sections, parts,
    top_grad, agg_in, pre_act, weights, local_adj_t, tiles, tile_source, owner_rows, counts,
):
    group_count, rows, feat = top_grad.shape
    assert group_count == 1
    slots = owner_rows.shape[3]
    tile_count, tile = tiles.shape[1], tiles.shape[2]
    chunk = min(128, feat)
    chunks = feat // chunk
    shard = feat // parts
    scale = 1.0 / math.sqrt(group_count * rows * parts)
    live = jnp.arange(slots)[None, :] < counts[0, 0][:, None]
    target = jnp.where(live, owner_rows[0, 0], rows).reshape(1, -1)
    wide = parts * slots
    bf16, f32 = jnp.bfloat16, jnp.float32
    dma = pltpu.SemaphoreType.DMA
    anywhere = pl.BlockSpec(memory_space=pl.ANY)
    vmem = pl.BlockSpec(memory_space=pltpu.VMEM)
    return pl.pallas_call(
        functools.partial(kernel, sections, parts, chunk, scale),
        out_shape=(
            jax.ShapeDtypeStruct((1, 1, rows, feat), bf16),
            jax.ShapeDtypeStruct((1, shard, feat), f32),
        ),
        in_specs=[anywhere] * 6 + [pl.BlockSpec(memory_space=pltpu.SMEM), vmem],
        out_specs=(vmem, vmem),
        scratch_shapes=[
            pltpu.VMEM((3, chunks, rows, chunk), bf16),
            pltpu.VMEM((2, rows, feat), bf16),
            pltpu.VMEM((2, feat, feat), bf16),
            pltpu.VMEM((rows, rows), bf16),
            pltpu.VMEM((rows, feat), bf16),
            pltpu.VMEM((tile_count, tile, tile), bf16),
            pltpu.VMEM((tile_count * tile, rows), bf16),
            pltpu.VMEM((rows, wide), bf16),
            pltpu.VMEM((rows, feat), bf16),
            pltpu.VMEM((rows, feat), f32),
            pltpu.VMEM((rows, feat), bf16),
            pltpu.VMEM((chunks, rows, chunk), f32),
            pltpu.VMEM((2, chunks, wide, chunk), bf16),
            pltpu.VMEM((2, chunks, wide, chunk), bf16),
            pltpu.VMEM((parts, shard, feat), bf16),
            pltpu.VMEM((shard, feat), f32),
            pltpu.VMEM((parts - 1, shard, feat), bf16),
            dma((5,)), dma((chunks,)), dma((chunks,)), dma((chunks,)), dma((2,)), dma((2,)),
            dma((2, chunks, parts - 1)), dma((2, chunks, parts - 1)),
            dma((parts - 1,)), dma((parts - 1,)),
        ],
        compiler_params=pltpu.CompilerParams(
            collective_id=0, has_side_effects=True, vmem_limit_bytes=50 * 1024 * 1024
        ),
    )(top_grad, agg_in, pre_act, weights, local_adj_t, tiles, tile_source, target)


def solution(mesh):
    in_specs = (
        P(None, "dom", None),
        P("section", None, "dom", None),
        P("section", None, "dom", None),
        P("section", None, None),
        P(None, "dom", None),
        P(None, "dom", None, None),
        P(None, "dom"),
        P(None, "dom", None, None),
        P(None, "dom", None),
    )
    out_specs = (P("section", None, "dom", None), P("section", "dom", None))
    return jax.shard_map(
        functools.partial(per_device, mesh.shape["section"], mesh.shape["dom"]),
        mesh=mesh, in_specs=in_specs, out_specs=out_specs, check_vma=False,
    )
```

```python
import functools
import math

import jax
import jax.numpy as jnp
from jax import lax
from jax.experimental import pallas as pl
from jax.experimental.pallas import tpu as pltpu
from jax.sharding import PartitionSpec as P

MESH = pl.DeviceIdType.MESH


def dot(a, b, dims=((1,), (0,))):
    return lax.dot_general(a, b, (dims, ((), ())), preferred_element_type=jnp.float32)


def kernel(
    sections, parts, chunk, scale,
    top, agg, pre, weight, adj, tiles, tile_source, owner_rows, counts,
    out_grad, out_dw,
    gbuf, pbuf, wbuf, abuf, xbuf, tbuf, tfull, sbuf, zbuf, yacc, ybuf, lbuf, msend, mrecv,
    dwfull, pairsend, pairrecv, chipsend, chiprecv, dwres,
    load_sem, first_sem, zin_sem, zout_sem, feed_out, feed_in, msend_sem, mrecv_sem,
    pair_out, pair_in, chip_out, chip_in, out_sem, dwout_sem,
):
    rows, feat = abuf.shape[0], zbuf.shape[1]
    chunks = feat // chunk
    slots = msend.shape[2] // parts
    tile_count, tile = tbuf.shape[0], tbuf.shape[1]
    shard = feat // parts
    sec = lax.axis_index("section")
    me = lax.axis_index("dom")
    top_sec = sections - 1
    is_top = sec == top_sec
    double = (lax.rem(sec, 2) == 0) & (sec < sections - 2)
    feeder = (lax.rem(sec, 2) == 1) & (sec < top_sec)
    passer = (sec > 0) & jnp.logical_not(feeder)
    begin = jnp.where(double, 0, 1)

    below = jnp.maximum(sec - 1, 0)
    below_slot = jnp.where((lax.rem(below, 2) == 0) & (below < sections - 2), 0, 1)

    loads = [
        pltpu.make_async_copy(weight.at[0], wbuf.at[1], load_sem.at[0]),
        pltpu.make_async_copy(pre.at[0, 0], pbuf.at[1], load_sem.at[1]),
        pltpu.make_async_copy(tiles.at[0], tbuf, load_sem.at[2]),
        pltpu.make_async_copy(adj.at[0], abuf, load_sem.at[3]),
        pltpu.make_async_copy(agg.at[0, 0], xbuf, load_sem.at[4]),
    ]

    def cols(c):
        return pl.ds(c * chunk, chunk)

    @pl.when(is_top)
    def _():
        for c in range(chunks):
            pltpu.make_async_copy(top.at[0, :, cols(c)], gbuf.at[1, c], first_sem.at[c]).start()

    for load in loads:
        load.start()

    barrier = pltpu.get_barrier_semaphore()
    for i in range(1, parts):
        pl.semaphore_signal(
            barrier, inc=1, device_id={"dom": lax.rem(me + i, parts)}, device_id_type=MESH
        )

    @pl.when(sec > 0)
    def _():
        pl.semaphore_signal(barrier, inc=1, device_id={"section": sec - 1}, device_id_type=MESH)

    @pl.when(sec < top_sec)
    def _():
        pl.semaphore_signal(barrier, inc=1, device_id={"section": sec + 1}, device_id_type=MESH)

    vertical = jnp.where(sec > 0, 1, 0) + jnp.where(sec < top_sec, 1, 0)
    pl.semaphore_wait(barrier, parts - 1 + vertical)

    def feed(i):
        source, dest = ((pre.at[0, 0], pbuf.at[0]), (weight.at[0], wbuf.at[0]))[i]
        return pltpu.make_async_remote_copy(
            src_ref=source, dst_ref=dest, send_sem=feed_out.at[i], recv_sem=feed_in.at[i],
            device_id={"section": below}, device_id_type=MESH,
        )

    @pl.when(feeder)
    def _():
        for i in range(2):
            feed(i).start()

    def pass_down(source_slot, c):
        return pltpu.make_async_remote_copy(
            src_ref=gbuf.at[source_slot, c], dst_ref=gbuf.at[below_slot, c],
            send_sem=zout_sem.at[c], recv_sem=zin_sem.at[c],
            device_id={"section": below}, device_id_type=MESH,
        )

    loads[2].wait()
    for b in range(tile_count):
        block = tbuf[b].astype(jnp.float32)
        for j in range(rows // tile):
            hit = (tile_source[0, b] == j).astype(jnp.float32)
            tfull[pl.ds(b * tile, tile), pl.ds(j * tile, tile)] = (block * hit).astype(jnp.bfloat16)
    loads[0].wait()
    loads[1].wait()
    loads[3].wait()

    def boundary_copy(phase, c, i):
        peer = lax.rem(me + i, parts)
        return pltpu.make_async_remote_copy(
            src_ref=msend.at[phase, c, pl.ds(pl.multiple_of(peer * slots, 16), slots)],
            dst_ref=mrecv.at[phase, c, pl.ds(pl.multiple_of(me * slots, 16), slots)],
            send_sem=msend_sem.at[phase, c, i - 1],
            recv_sem=mrecv_sem.at[phase, c, i - 1],
            device_id={"dom": peer}, device_id_type=MESH,
        )

    def boundary_arrived(phase, c, i):
        source = lax.rem(me + parts - i, parts)
        return pltpu.make_async_remote_copy(
            src_ref=msend.at[phase, c, pl.ds(pl.multiple_of(source * slots, 16), slots)],
            dst_ref=mrecv.at[phase, c, pl.ds(pl.multiple_of(source * slots, 16), slots)],
            send_sem=msend_sem.at[phase, c, i - 1],
            recv_sem=mrecv_sem.at[phase, c, i - 1],
            device_id={"dom": source}, device_id_type=MESH,
        )

    core = lax.rem(me, 2)
    partner = me + 1 - 2 * core
    here = (me - core) // 2
    chips = parts // 2

    def shard_at(index):
        return pl.ds(pl.multiple_of(index * shard, shard), shard)

    def pair_copy():
        return pltpu.make_async_remote_copy(
            src_ref=pairsend, dst_ref=pairrecv, send_sem=pair_out, recv_sem=pair_in,
            device_id={"dom": partner}, device_id_type=MESH,
        )

    def chip_copy(i):
        peer = 2 * lax.rem(here + i, chips) + core
        return pltpu.make_async_remote_copy(
            src_ref=chipsend.at[i - 1], dst_ref=chiprecv.at[i - 1],
            send_sem=chip_out.at[i - 1], recv_sem=chip_in.at[i - 1],
            device_id={"dom": peer}, device_id_type=MESH,
        )

    def weight_terms():
        dwfull[...] = dot(xbuf[...], zbuf[...], ((0,), (0,)))
        for j in range(chips):
            pairsend[j] = dwfull[shard_at(2 * j + 1 - core), :].astype(jnp.bfloat16)
        pair_copy().start()

    def weight_sums():
        pair_copy().wait_recv()
        for i in range(1, chips):
            j = lax.rem(here + i, chips)
            both = dwfull[shard_at(2 * j + core), :] + pairrecv[j].astype(jnp.float32)
            chipsend[i - 1] = both.astype(jnp.bfloat16)
            chip_copy(i).start()
        dwres[...] = dwfull[shard_at(me), :] + pairrecv[here].astype(jnp.float32)

    spot = lax.broadcasted_iota(jnp.int32, (rows, parts * slots), 0)
    slot = lax.broadcasted_iota(jnp.int32, (1, slots), 1)
    target = jnp.concatenate(
        [
            jnp.where(slot < counts[0, 0, d], owner_rows[0, 0, pl.ds(d, 1), :], rows)
            for d in range(parts)
        ],
        axis=1,
    )
    sbuf[...] = jnp.where(spot == target, 1.0, 0.0).astype(jnp.bfloat16)

    def front(phase, c, gradient):
        keep = pbuf[phase, :, cols(c)].astype(jnp.float32) > 0
        masked = jnp.where(keep, gradient.astype(jnp.float32), 0.0).astype(jnp.bfloat16)
        zbuf[:, cols(c)] = masked
        term = dot(masked, wbuf[phase, :, cols(c)], ((1,), (1,)))
        if c == 0:
            yacc[...] = term
        elif c < chunks - 1:
            yacc[...] += term
        else:
            ybuf[...] = (yacc[...] + term).astype(jnp.bfloat16)

    def out_copy(c):
        return pltpu.make_async_copy(
            gbuf.at[2, c], out_grad.at[0, 0, :, cols(c)], out_sem.at[c]
        )

    @pl.when(double)
    def _():
        for i in range(2):
            feed(i).wait_recv()

    for c in range(chunks):
        @pl.when(jnp.logical_not(is_top))
        def _():
            pass_down(1, c).wait_recv()

        @pl.when(is_top)
        def _():
            pltpu.make_async_copy(
                top.at[0, :, cols(c)], gbuf.at[1, c], first_sem.at[c]
            ).wait()

        @pl.when(feeder)
        def _():
            pass_down(1, c).start()

        front(begin, c, gbuf[begin, c])

    def run_layer(phase, carry):
        for c in range(chunks):
            msend[phase, c] = dot(tfull[...], ybuf[:, cols(c)]).astype(jnp.bfloat16)
            for i in range(1, parts):
                boundary_copy(phase, c, i).start()
            own = pl.ds(pl.multiple_of(me * slots, 16), slots)
            mrecv[phase, c, own, :] = msend[phase, c, own, :]

        last = phase == 1

        @pl.when(last & jnp.logical_not(passer))
        def _():
            loads[4].wait()
            weight_terms()

        for c in range(chunks):
            lbuf[c] = dot(abuf[...], ybuf[:, cols(c)])

        @pl.when(last & jnp.logical_not(passer))
        def _():
            weight_sums()

        for c in range(chunks):
            for i in range(1, parts):
                boundary_arrived(phase, c, i).wait_recv()
            total = (lbuf[c] + dot(sbuf[...], mrecv[phase, c])).astype(jnp.bfloat16)
            gbuf[phase + 1, c] = total

            @pl.when(last)
            def _():
                @pl.when(passer)
                def _():
                    pass_down(2, c).start()

                out_copy(c).start()

            @pl.when(jnp.logical_not(last))
            def _():
                front(1, c, total)

        return carry

    lax.fori_loop(begin, 2, run_layer, 0)

    @pl.when(passer)
    def _():
        loads[4].wait()
        weight_terms()
        weight_sums()

    total = dwres[...]
    for i in range(1, chips):
        chip_copy(i).wait_recv()
        total = total + chiprecv[i - 1].astype(jnp.float32)
    dwres[...] = total * scale
    dwout = pltpu.make_async_copy(dwres, out_dw.at[0], dwout_sem)
    dwout.start()

    pair_copy().wait_send()
    for i in range(1, chips):
        chip_copy(i).wait_send()

    @pl.when(sec > 0)
    def _():
        for c in range(chunks):
            pass_down(1, c).wait_send()

    @pl.when(feeder)
    def _():
        for i in range(2):
            feed(i).wait_send()

    def drain(phase):
        for c in range(chunks):
            for i in range(1, parts):
                boundary_copy(phase, c, i).wait_send()

    @pl.when(double)
    def _():
        drain(0)

    drain(1)
    for c in range(chunks):
        out_copy(c).wait()
    dwout.wait()


def per_device(
    sections, parts,
    top_grad, agg_in, pre_act, weights, local_adj_t, tiles, tile_source, owner_rows, counts,
):
    group_count, rows, feat = top_grad.shape
    assert group_count == 1
    slots = owner_rows.shape[3]
    tile_count, tile = tiles.shape[1], tiles.shape[2]
    chunk = min(128, feat)
    chunks = feat // chunk
    shard = feat // parts
    scale = 1.0 / math.sqrt(group_count * rows * parts)
    wide = parts * slots
    bf16, f32 = jnp.bfloat16, jnp.float32
    dma = pltpu.SemaphoreType.DMA
    anywhere = pl.BlockSpec(memory_space=pl.ANY)
    vmem = pl.BlockSpec(memory_space=pltpu.VMEM)
    smem = pl.BlockSpec(memory_space=pltpu.SMEM)
    return pl.pallas_call(
        functools.partial(kernel, sections, parts, chunk, scale),
        out_shape=(
            jax.ShapeDtypeStruct((1, 1, rows, feat), bf16),
            jax.ShapeDtypeStruct((1, shard, feat), f32),
        ),
        in_specs=[anywhere] * 6 + [smem, vmem, smem],
        out_specs=(anywhere, anywhere),
        scratch_shapes=[
            pltpu.VMEM((3, chunks, rows, chunk), bf16),
            pltpu.VMEM((2, rows, feat), bf16),
            pltpu.VMEM((2, feat, feat), bf16),
            pltpu.VMEM((rows, rows), bf16),
            pltpu.VMEM((rows, feat), bf16),
            pltpu.VMEM((tile_count, tile, tile), bf16),
            pltpu.VMEM((tile_count * tile, rows), bf16),
            pltpu.VMEM((rows, wide), bf16),
            pltpu.VMEM((rows, feat), bf16),
            pltpu.VMEM((rows, feat), f32),
            pltpu.VMEM((rows, feat), bf16),
            pltpu.VMEM((chunks, rows, chunk), f32),
            pltpu.VMEM((2, chunks, wide, chunk), bf16),
            pltpu.VMEM((2, chunks, wide, chunk), bf16),
            pltpu.VMEM((feat, feat), f32),
            pltpu.VMEM((parts // 2, shard, feat), bf16),
            pltpu.VMEM((parts // 2, shard, feat), bf16),
            pltpu.VMEM((parts // 2 - 1, shard, feat), bf16),
            pltpu.VMEM((parts // 2 - 1, shard, feat), bf16),
            pltpu.VMEM((shard, feat), f32),
            dma((5,)), dma((chunks,)), dma((chunks,)), dma((chunks,)), dma((2,)), dma((2,)),
            dma((2, chunks, parts - 1)), dma((2, chunks, parts - 1)),
            dma, dma, dma((parts // 2 - 1,)), dma((parts // 2 - 1,)), dma((chunks,)), dma,
        ],
        compiler_params=pltpu.CompilerParams(
            collective_id=0, has_side_effects=True, vmem_limit_bytes=60 * 1024 * 1024
        ),
    )(
        top_grad, agg_in, pre_act, weights, local_adj_t, tiles, tile_source, owner_rows, counts
    )


def solution(mesh):
    in_specs = (
        P(None, "dom", None),
        P("section", None, "dom", None),
        P("section", None, "dom", None),
        P("section", None, None),
        P(None, "dom", None),
        P(None, "dom", None, None),
        P(None, "dom"),
        P(None, "dom", None, None),
        P(None, "dom", None),
    )
    out_specs = (P("section", None, "dom", None), P("section", "dom", None))
    return jax.shard_map(
        functools.partial(per_device, mesh.shape["section"], mesh.shape["dom"]),
        mesh=mesh, in_specs=in_specs, out_specs=out_specs, check_vma=False,
    )
```

```python
import functools
import math

import jax
import jax.numpy as jnp
from jax import lax
from jax.experimental import pallas as pl
from jax.experimental.pallas import tpu as pltpu
from jax.sharding import PartitionSpec as P

MESH = pl.DeviceIdType.MESH


def dot(a, b, dims=((1,), (0,))):
    return lax.dot_general(a, b, (dims, ((), ())), preferred_element_type=jnp.float32)


def kernel(
    sections, parts, chunk, pieces, scale,
    top, agg, pre, weight, adj, tiles, tile_source, owner_rows, counts,
    out_grad, out_dw,
    gbuf, pbuf, wbuf, abuf, xbuf, tbuf, tfull, sbuf, zbuf, yacc, ybuf, lbuf, msend, mrecv,
    dwfull, pairsend, pairrecv, chipsend, chiprecv, dwres,
    load_sem, first_sem, zin_sem, zout_sem, feed_out, feed_in, msend_sem, mrecv_sem,
    pair_out, pair_in, chip_out, chip_in, out_sem, dwout_sem,
):
    rows, feat = abuf.shape[0], zbuf.shape[1]
    chunks = feat // chunk
    slots = msend.shape[2] // parts
    tile_count, tile = tbuf.shape[0], tbuf.shape[1]
    shard = feat // parts
    sec = lax.axis_index("section")
    me = lax.axis_index("dom")
    top_sec = sections - 1
    is_top = sec == top_sec
    double = (lax.rem(sec, 2) == 0) & (sec < sections - 2)
    feeder = (lax.rem(sec, 2) == 1) & (sec < top_sec)
    passer = (sec > 0) & jnp.logical_not(feeder)
    begin = jnp.where(double, 0, 1)

    below = jnp.maximum(sec - 1, 0)
    below_slot = jnp.where((lax.rem(below, 2) == 0) & (below < sections - 2), 0, 1)

    loads = [
        pltpu.make_async_copy(weight.at[0], wbuf.at[1], load_sem.at[0]),
        pltpu.make_async_copy(pre.at[0, 0], pbuf.at[1], load_sem.at[1]),
        pltpu.make_async_copy(tiles.at[0], tbuf, load_sem.at[2]),
        pltpu.make_async_copy(adj.at[0], abuf, load_sem.at[3]),
        pltpu.make_async_copy(agg.at[0, 0], xbuf, load_sem.at[4]),
    ]

    def cols(c):
        return pl.ds(c * chunk, chunk)

    barrier = pltpu.get_barrier_semaphore()
    for i in range(1, parts):
        pl.semaphore_signal(
            barrier, inc=1, device_id={"dom": lax.rem(me + i, parts)}, device_id_type=MESH
        )

    @pl.when(sec > 0)
    def _():
        pl.semaphore_signal(barrier, inc=1, device_id={"section": sec - 1}, device_id_type=MESH)

    @pl.when(sec < top_sec)
    def _():
        pl.semaphore_signal(barrier, inc=1, device_id={"section": sec + 1}, device_id_type=MESH)

    @pl.when(is_top)
    def _():
        for c in range(chunks):
            pltpu.make_async_copy(top.at[0, :, cols(c)], gbuf.at[1, c], first_sem.at[c]).start()

    for load in loads:
        load.start()

    def feed(i):
        source, dest = ((pre.at[0, 0], pbuf.at[0]), (weight.at[0], wbuf.at[0]))[i]
        return pltpu.make_async_remote_copy(
            src_ref=source, dst_ref=dest, send_sem=feed_out.at[i], recv_sem=feed_in.at[i],
            device_id={"section": below}, device_id_type=MESH,
        )

    def pass_down(source_slot, c, r):
        piece = pl.ds(r * (rows // pieces), rows // pieces)
        return pltpu.make_async_remote_copy(
            src_ref=gbuf.at[source_slot, c, piece], dst_ref=gbuf.at[below_slot, c, piece],
            send_sem=zout_sem.at[c, r], recv_sem=zin_sem.at[c, r],
            device_id={"section": below}, device_id_type=MESH,
        )

    loads[2].wait()
    for b in range(tile_count):
        block = tbuf[b].astype(jnp.float32)
        for j in range(rows // tile):
            hit = (tile_source[0, b] == j).astype(jnp.float32)
            tfull[pl.ds(b * tile, tile), pl.ds(j * tile, tile)] = (block * hit).astype(jnp.bfloat16)
    spot = lax.broadcasted_iota(jnp.int32, (rows, parts * slots), 0)
    slot = lax.broadcasted_iota(jnp.int32, (1, slots), 1)
    target = jnp.concatenate(
        [
            jnp.where(slot < counts[0, 0, d], owner_rows[0, 0, pl.ds(d, 1), :], rows)
            for d in range(parts)
        ],
        axis=1,
    )
    sbuf[...] = jnp.where(spot == target, 1.0, 0.0).astype(jnp.bfloat16)

    vertical = jnp.where(sec > 0, 1, 0) + jnp.where(sec < top_sec, 1, 0)
    pl.semaphore_wait(barrier, parts - 1 + vertical)

    @pl.when(feeder)
    def _():
        for i in range(2):
            feed(i).start()

    loads[0].wait()
    loads[1].wait()
    loads[3].wait()

    def boundary_copy(phase, c, i):
        peer = lax.rem(me + i, parts)
        return pltpu.make_async_remote_copy(
            src_ref=msend.at[phase, c, pl.ds(pl.multiple_of(peer * slots, 16), slots)],
            dst_ref=mrecv.at[phase, c, pl.ds(pl.multiple_of(me * slots, 16), slots)],
            send_sem=msend_sem.at[phase, c, i - 1],
            recv_sem=mrecv_sem.at[phase, c, i - 1],
            device_id={"dom": peer}, device_id_type=MESH,
        )

    def boundary_arrived(phase, c, i):
        source = lax.rem(me + parts - i, parts)
        return pltpu.make_async_remote_copy(
            src_ref=msend.at[phase, c, pl.ds(pl.multiple_of(source * slots, 16), slots)],
            dst_ref=mrecv.at[phase, c, pl.ds(pl.multiple_of(source * slots, 16), slots)],
            send_sem=msend_sem.at[phase, c, i - 1],
            recv_sem=mrecv_sem.at[phase, c, i - 1],
            device_id={"dom": source}, device_id_type=MESH,
        )

    core = lax.rem(me, 2)
    partner = me + 1 - 2 * core
    here = (me - core) // 2
    chips = parts // 2

    def shard_at(index):
        return pl.ds(pl.multiple_of(index * shard, shard), shard)

    def pair_copy():
        return pltpu.make_async_remote_copy(
            src_ref=pairsend, dst_ref=pairrecv, send_sem=pair_out, recv_sem=pair_in,
            device_id={"dom": partner}, device_id_type=MESH,
        )

    def chip_copy(i):
        peer = 2 * lax.rem(here + i, chips) + core
        return pltpu.make_async_remote_copy(
            src_ref=chipsend.at[i - 1], dst_ref=chiprecv.at[i - 1],
            send_sem=chip_out.at[i - 1], recv_sem=chip_in.at[i - 1],
            device_id={"dom": peer}, device_id_type=MESH,
        )

    def weight_terms():
        dwfull[...] = dot(xbuf[...], zbuf[...], ((0,), (0,)))
        for j in range(chips):
            pairsend[j] = dwfull[shard_at(2 * j + 1 - core), :].astype(jnp.bfloat16)
        pair_copy().start()

    def weight_sums():
        pair_copy().wait_recv()
        for i in range(1, chips):
            j = lax.rem(here + i, chips)
            both = dwfull[shard_at(2 * j + core), :] + pairrecv[j].astype(jnp.float32)
            chipsend[i - 1] = both.astype(jnp.bfloat16)
            chip_copy(i).start()
        dwres[...] = dwfull[shard_at(me), :] + pairrecv[here].astype(jnp.float32)

    def front(phase, c, gradient):
        keep = pbuf[phase, :, cols(c)].astype(jnp.float32) > 0
        masked = jnp.where(keep, gradient.astype(jnp.float32), 0.0).astype(jnp.bfloat16)
        zbuf[:, cols(c)] = masked
        term = dot(masked, wbuf[phase, :, cols(c)], ((1,), (1,)))
        if c == 0:
            yacc[...] = term
        elif c < chunks - 1:
            yacc[...] += term
        else:
            ybuf[...] = (yacc[...] + term).astype(jnp.bfloat16)

    def out_copy(c):
        return pltpu.make_async_copy(
            gbuf.at[2, c], out_grad.at[0, 0, :, cols(c)], out_sem.at[c]
        )

    @pl.when(double)
    def _():
        for i in range(2):
            feed(i).wait_recv()

    for c in range(chunks):
        for r in range(pieces):
            @pl.when(jnp.logical_not(is_top))
            def _():
                pass_down(1, c, r).wait_recv()

            @pl.when(feeder)
            def _():
                pass_down(1, c, r).start()

        @pl.when(is_top)
        def _():
            pltpu.make_async_copy(
                top.at[0, :, cols(c)], gbuf.at[1, c], first_sem.at[c]
            ).wait()

        front(begin, c, gbuf[begin, c])

    def run_layer(phase, carry):
        for c in range(chunks):
            msend[phase, c] = dot(tfull[...], ybuf[:, cols(c)]).astype(jnp.bfloat16)
            for i in range(1, parts):
                boundary_copy(phase, c, i).start()
            own = pl.ds(pl.multiple_of(me * slots, 16), slots)
            mrecv[phase, c, own, :] = msend[phase, c, own, :]

        last = phase == 1

        @pl.when(last & jnp.logical_not(passer))
        def _():
            loads[4].wait()
            weight_terms()

        for c in range(chunks):
            lbuf[c] = dot(abuf[...], ybuf[:, cols(c)])

        @pl.when(last & jnp.logical_not(passer))
        def _():
            weight_sums()

        for c in range(chunks):
            for i in range(1, parts):
                boundary_arrived(phase, c, i).wait_recv()
            total = (lbuf[c] + dot(sbuf[...], mrecv[phase, c])).astype(jnp.bfloat16)
            gbuf[phase + 1, c] = total

            @pl.when(last)
            def _():
                @pl.when(passer)
                def _():
                    for r in range(pieces):
                        pass_down(2, c, r).start()

                out_copy(c).start()

            @pl.when(jnp.logical_not(last))
            def _():
                front(1, c, total)

        return carry

    lax.fori_loop(begin, 2, run_layer, 0)

    @pl.when(passer)
    def _():
        loads[4].wait()
        weight_terms()
        weight_sums()

    total = dwres[...]
    for i in range(1, chips):
        chip_copy(i).wait_recv()
        total = total + chiprecv[i - 1].astype(jnp.float32)
    dwres[...] = total * scale
    dwout = pltpu.make_async_copy(dwres, out_dw.at[0], dwout_sem)
    dwout.start()

    pair_copy().wait_send()
    for i in range(1, chips):
        chip_copy(i).wait_send()

    @pl.when(sec > 0)
    def _():
        for c in range(chunks):
            for r in range(pieces):
                pass_down(1, c, r).wait_send()

    @pl.when(feeder)
    def _():
        for i in range(2):
            feed(i).wait_send()

    def drain(phase):
        for c in range(chunks):
            for i in range(1, parts):
                boundary_copy(phase, c, i).wait_send()

    @pl.when(double)
    def _():
        drain(0)

    drain(1)
    for c in range(chunks):
        out_copy(c).wait()
    dwout.wait()


def per_device(
    sections, parts,
    top_grad, agg_in, pre_act, weights, local_adj_t, tiles, tile_source, owner_rows, counts,
):
    group_count, rows, feat = top_grad.shape
    assert group_count == 1
    slots = owner_rows.shape[3]
    tile_count, tile = tiles.shape[1], tiles.shape[2]
    chunk = min(128, feat)
    chunks = feat // chunk
    pieces = 4
    shard = feat // parts
    scale = 1.0 / math.sqrt(group_count * rows * parts)
    wide = parts * slots
    bf16, f32 = jnp.bfloat16, jnp.float32
    dma = pltpu.SemaphoreType.DMA
    anywhere = pl.BlockSpec(memory_space=pl.ANY)
    vmem = pl.BlockSpec(memory_space=pltpu.VMEM)
    smem = pl.BlockSpec(memory_space=pltpu.SMEM)
    return pl.pallas_call(
        functools.partial(kernel, sections, parts, chunk, pieces, scale),
        out_shape=(
            jax.ShapeDtypeStruct((1, 1, rows, feat), bf16),
            jax.ShapeDtypeStruct((1, shard, feat), f32),
        ),
        in_specs=[anywhere] * 6 + [smem, vmem, smem],
        out_specs=(anywhere, anywhere),
        scratch_shapes=[
            pltpu.VMEM((3, chunks, rows, chunk), bf16),
            pltpu.VMEM((2, rows, feat), bf16),
            pltpu.VMEM((2, feat, feat), bf16),
            pltpu.VMEM((rows, rows), bf16),
            pltpu.VMEM((rows, feat), bf16),
            pltpu.VMEM((tile_count, tile, tile), bf16),
            pltpu.VMEM((tile_count * tile, rows), bf16),
            pltpu.VMEM((rows, wide), bf16),
            pltpu.VMEM((rows, feat), bf16),
            pltpu.VMEM((rows, feat), f32),
            pltpu.VMEM((rows, feat), bf16),
            pltpu.VMEM((chunks, rows, chunk), f32),
            pltpu.VMEM((2, chunks, wide, chunk), bf16),
            pltpu.VMEM((2, chunks, wide, chunk), bf16),
            pltpu.VMEM((feat, feat), f32),
            pltpu.VMEM((parts // 2, shard, feat), bf16),
            pltpu.VMEM((parts // 2, shard, feat), bf16),
            pltpu.VMEM((parts // 2 - 1, shard, feat), bf16),
            pltpu.VMEM((parts // 2 - 1, shard, feat), bf16),
            pltpu.VMEM((shard, feat), f32),
            dma((5,)), dma((chunks,)), dma((chunks, pieces)), dma((chunks, pieces)), dma((2,)), dma((2,)),
            dma((2, chunks, parts - 1)), dma((2, chunks, parts - 1)),
            dma, dma, dma((parts // 2 - 1,)), dma((parts // 2 - 1,)), dma((chunks,)), dma,
        ],
        compiler_params=pltpu.CompilerParams(
            collective_id=0, has_side_effects=True, vmem_limit_bytes=60 * 1024 * 1024
        ),
    )(
        top_grad, agg_in, pre_act, weights, local_adj_t, tiles, tile_source, owner_rows, counts
    )


def solution(mesh):
    in_specs = (
        P(None, "dom", None),
        P("section", None, "dom", None),
        P("section", None, "dom", None),
        P("section", None, None),
        P(None, "dom", None),
        P(None, "dom", None, None),
        P(None, "dom"),
        P(None, "dom", None, None),
        P(None, "dom", None),
    )
    out_specs = (P("section", None, "dom", None), P("section", "dom", None))
    return jax.shard_map(
        functools.partial(per_device, mesh.shape["section"], mesh.shape["dom"]),
        mesh=mesh, in_specs=in_specs, out_specs=out_specs, check_vma=False,
    )
```
